512 devices in a mesh: section: 4 (over z_hi), dp: 8 (over x, core), tensor: 16 (over z_lo, y).
Axes of the slice: x: 4, y: 4, z: 16 (z_hi: 4, z_lo: 4; z = z_hi * 4 + z_lo), core: 2. Of those that a mesh axis runs over, the one named last changes fastest.
Arguments:
- hidden: bfloat16 [4, 1024, 28672], P('section', 'tensor', 'dp'), may hold values from -6 to 6
- down_weight: bfloat16 [4, 28672, 8192], P('section', 'dp', 'tensor'), may hold values from -0.03125 to 0.03125
- residual: bfloat16 [4, 1024, 8192], P('section', 'dp', 'tensor'), may hold values from -36 to 36
- norm_gain: float32 [4, 8192], P('section', 'tensor'), may hold values from 0.4 to 1.2
- query_weight: bfloat16 [4, 8192, 4096], P('section', 'tensor', 'dp'), may hold values from -0.0625 to 0.0625
- key_value_weight: bfloat16 [4, 8192, 2048], P('section', 'tensor', 'dp'), may hold values from -0.0625 to 0.0625
Outputs:
- attention: bfloat16 [4, 1024, 4096], P('section', 'tensor', 'dp')
The draws below stay inside these ranges and needn't reach their ends.
All inputs are finite; a program needn't handle non-finite values.
Results may differ from the reference program's by a relative error of at most 0.04.
Values may be sent and summed in bfloat16 or wider, within the bound.
A program may use at most 64 MiB of HBM per device.

```python
import math
import jax
import jax.numpy as jnp
from jax import lax

D = 8192
FF = 28672
HD = 128
QH = 32
KVH = 8
SEQ = 1024
SECTIONS = 4
N_DP = 8


def log_scales(key, shape, lower, upper):
    return jnp.exp(jax.random.uniform(key, shape, jnp.float32, math.log(lower), math.log(upper)))


def draw_residual(key, part):
    base_key = jax.random.fold_in(key, 11)
    noise = jax.random.truncated_normal(jax.random.fold_in(base_key, 1), -4.0, 4.0, (SECTIONS, SEQ, D), jnp.float32)
    row_scale = log_scales(jax.random.fold_in(base_key, 2), (SECTIONS, SEQ, 1), 0.3, 3.0)
    column_scale = log_scales(jax.random.fold_in(base_key, 3), (SECTIONS, 1, D), 0.3, 3.0)
    return (noise * row_scale * column_scale).astype(jnp.bfloat16)


def draw_norm_gain(key, part):
    base_key = jax.random.fold_in(key, 23)
    return log_scales(base_key, (SECTIONS, D), 0.4, 1.2)


def with_spikes(entries, own_key, source, target, blocks, factor):
    owner, partner = [(jnp.arange(entries.shape[position]) // (entries.shape[position] // blocks)).reshape([-1 if axis == position else 1 for axis in range(entries.ndim)]) for position in (source, target)]
    chosen = jax.random.permutation(own_key, blocks)[partner]
    strong = (owner == chosen) | (owner == (partner + blocks // 2) % blocks)
    return jnp.where(strong, factor * entries, entries)


def level_of(key, dims, split, least, largest):
    level = 1.0
    for axis_at, parts in split:
        heights = jax.random.uniform(jax.random.fold_in(jax.random.fold_in(key, 6), axis_at), (parts,), jnp.float32, least / len(split), largest / len(split))
        level = level * jnp.repeat(jnp.exp(heights), dims[axis_at] // parts).reshape((-1,) + (1,) * (len(dims) - 1 - axis_at))
    return level


def normal_values(stream_key, extent, deviation, limit, split=(), held_as=jnp.bfloat16):
    level = level_of(stream_key, extent, split, -0.22, 0.18) if split else 1.0
    values = jax.random.normal(stream_key, extent, jnp.float32) * deviation * level
    return jnp.minimum(jnp.maximum(values, -limit), limit).astype(held_as)


def heavy_noise(rng, shape, deviation, limit, split, heavy, held_as=jnp.bfloat16):
    drawn = deviation * jax.random.normal(rng, shape, jnp.float32)
    if split:
        drawn = drawn * level_of(rng, shape, split, -0.22, 0.18)
    return jnp.clip(with_spikes(drawn, jax.random.fold_in(rng, 3), *heavy), -limit, limit).astype(held_as)


def setup_inputs(seed: int = 0) -> dict:
    key_of = jax.random.split(jax.random.key(seed), 7)
    hidden = heavy_noise(key_of[0], (SECTIONS, SEQ, FF), 1.0, 6.0, ((0, 4), (1, 16), (2, 8)), (2, 1, 16, 2.0))
    down_weight = normal_values(key_of[1], (SECTIONS, FF, D), FF ** -0.5, 0.03125, ((0, 4), (1, 8), (2, 16)))
    residual = draw_residual(jax.random.fold_in(key_of[6], 71), 0)
    norm_gain = draw_norm_gain(jax.random.fold_in(key_of[6], 71), 0)
    query_weight = normal_values(key_of[4], (SECTIONS, D, QH * HD), D ** -0.5, 0.0625, ((0, 4), (1, 16), (2, 8)))
    key_value_weight = normal_values(key_of[5], (SECTIONS, D, KVH * 2 * HD), D ** -0.5, 0.0625, ((0, 4), (1, 16), (2, 8)))
    return dict(hidden=hidden, down_weight=down_weight, residual=residual, norm_gain=norm_gain, query_weight=query_weight, key_value_weight=key_value_weight)


ROPE_BASE = 500000.0
EPSILON = 1e-05

def rotate(values, positions):
    half_dim = values.shape[-1] // 2
    frequency = ROPE_BASE ** (-jnp.arange(half_dim, dtype=jnp.float32) * 2.0 / values.shape[-1])
    angles = positions.astype(jnp.float32)[:, None] * frequency[None, :]
    cosine = jnp.cos(angles)[:, None, :]
    sine_part = jnp.sin(angles)[:, None, :]
    front_part = values[..., :half_dim]
    back_part = values[..., half_dim:]
    return jnp.concatenate([front_part * cosine - back_part * sine_part, back_part * cosine + front_part * sine_part], axis=-1)

def boundary_of(hidden, down_weight, residual, section_index):
    block_width = FF // N_DP
    summed = jnp.zeros((SEQ, D), jnp.float32)
    for block_index in range(N_DP):
        lower = block_index * block_width
        partial_value = jnp.dot(hidden[section_index][:, lower:lower + block_width], down_weight[section_index][lower:lower + block_width], preferred_element_type=jnp.float32)
        rounded = lax.optimization_barrier(partial_value.astype(jnp.bfloat16))
        summed = summed + rounded.astype(jnp.float32)
    return (residual[section_index].astype(jnp.float32) + summed).astype(jnp.bfloat16)

def attend(arrived, norm_gain, query_weight, key_value_weight):
    values_in = arrived.astype(jnp.float32)
    inverse = lax.rsqrt(lax.optimization_barrier(jnp.mean(values_in * values_in, axis=1, keepdims=True)) + EPSILON)
    scaled = (values_in * norm_gain[None, :]).astype(jnp.bfloat16)
    query_sums = jnp.dot(scaled, query_weight, preferred_element_type=jnp.float32) * inverse
    pair_sums = jnp.dot(scaled, key_value_weight, preferred_element_type=jnp.float32) * inverse
    positions = jnp.arange(SEQ, dtype=jnp.int32)
    queries = rotate(query_sums.reshape(SEQ, QH, HD), positions).astype(jnp.bfloat16)
    pair_rows = pair_sums.reshape(SEQ, KVH, 2, HD)
    key_rows = rotate(pair_rows[:, :, 0], positions).astype(jnp.bfloat16)
    value_rows = pair_rows[:, :, 1].astype(jnp.bfloat16)
    group_ratio = QH // KVH
    grouped = queries.reshape(SEQ, KVH, group_ratio, HD)
    causal = positions[None, :] <= positions[:, None]

    def one_group(group_index):
        query_block = grouped[:, group_index].astype(jnp.float32)
        scores = jnp.einsum('qrd,kd->rqk', query_block, key_rows[:, group_index].astype(jnp.float32)) * HD ** (-0.5)
        scores = jnp.where(causal[None], scores, -1e+30)
        maximum = lax.optimization_barrier(jnp.max(scores, axis=-1, keepdims=True))
        weights = jnp.exp(scores - maximum)
        probabilities = (weights / lax.optimization_barrier(jnp.sum(weights, axis=-1, keepdims=True))).astype(jnp.bfloat16)
        return jnp.einsum('rqk,kd->qrd', probabilities.astype(jnp.float32), value_rows[:, group_index].astype(jnp.float32)).astype(jnp.bfloat16)
    outputs = lax.map(one_group, jnp.arange(KVH, dtype=jnp.int32))
    return jnp.transpose(outputs, (1, 0, 2, 3)).reshape(SEQ, QH * HD)

def reference(hidden, down_weight, residual, norm_gain, query_weight, key_value_weight):
    boundaries = [boundary_of(hidden, down_weight, residual, section_index) for section_index in range(SECTIONS)]
    results = []
    for section_index in range(SECTIONS):
        arrived = boundaries[(section_index - 1) % SECTIONS]
        results.append(attend(arrived, norm_gain[section_index], query_weight[section_index], key_value_weight[section_index]))
    return jnp.stack(results)
```

```python
import jax
import jax.numpy as jnp
from jax import lax
from jax.experimental import pallas as pl
from jax.experimental.pallas import tpu as pltpu
from jax.sharding import PartitionSpec as P

D = 8192
HD = 128
ROPE_BASE = 500000.0
EPSILON = 1e-05

MESH = pl.DeviceIdType.MESH
NZ, NY, ND, NS = 4, 4, 8, 4
NK = 4
ROWS = 16
BF = jnp.bfloat16
F32 = jnp.float32


def kernel(
    hid, w_hbm, wq_hbm, wkv_hbm, res, gain, ctab, stab, out,
    G, W, WP, acc, Pb, R, B, E, U, RY, V, RZ, SQ, SY, SV, SZ, Qb, KV,
    lsem, zsnd, zrcv, ysnd, yrcv, fsnd, frcv, dsnd, drcv, ssnd, srcv, gsnd, grcv,
    usnd, urcv, vsnd, vrcv, qysnd, qyrcv, qzsnd, qzrcv, kzsnd, kzrcv, kysnd, kyrcv,
):
    s = lax.axis_index("section")
    d = lax.axis_index("dp")
    t = lax.axis_index("tensor")
    z, y = t // NY, t % NY
    ff, feats = W.shape
    half = ff // 2
    inner = jnp.logical_and(z > 0, z < NZ - 1)

    def at_z(zz):
        return (s, d, zz * NY + y)

    def at_y(yy):
        return (s, d, z * NY + yy)

    def at_d(dd):
        return (s, dd, t)

    def piece(i):
        return (z, z + 1 - 2 * (z % 2), 2 - z // 2, 3 - 3 * (z // 2))[i]

    def remote(src, dst, snd, rcv, where):
        return pltpu.make_async_remote_copy(
            src_ref=src, dst_ref=dst, send_sem=snd, recv_sem=rcv, device_id=where, device_id_type=MESH
        )

    sent = []

    def send(copy, cond=None):
        if cond is None:
            copy.start()
        else:
            pl.when(cond)(copy.start)
        sent.append((cond, copy))

    local = [
        pltpu.make_async_copy(hid, G.at[:, y, z], lsem.at[0]),
        pltpu.make_async_copy(w_hbm, W, lsem.at[1]),
        pltpu.make_async_copy(wq_hbm, WP.at[:, pl.ds(0, 512)], lsem.at[2]),
        pltpu.make_async_copy(wkv_hbm, WP.at[:, pl.ds(512, 256)], lsem.at[3]),
    ]
    for copy in local:
        copy.start()

    barrier = pltpu.get_barrier_semaphore()
    peers = [at_y((y + j) % NY) for j in range(1, NY)]
    peers += [at_z((z + j) % NZ) for j in range(1, NZ)]
    peers += [at_d((d + j) % ND) for j in range(1, ND)]
    peers += [((s + 1) % NS, d, t), ((s + NS - 1) % NS, d, t)]
    for peer in peers:
        pl.semaphore_signal(barrier, inc=1, device_id=peer, device_id_type=MESH)
    pl.semaphore_wait(barrier, len(peers))
    local[0].wait()

    up, down = (y + 1) % NY, (y + NY - 1) % NY

    def gather_z(k, i):
        zp = piece(i)
        own = G.at[k, y, zp]
        if i == 0:
            send(remote(own, own, zsnd.at[k, 0], zrcv.at[k, zp], at_z(jnp.minimum(z + 1, NZ - 1))), z < NZ - 1)
            send(remote(own, own, zsnd.at[k, 1], zrcv.at[k, zp], at_z(jnp.maximum(z - 1, 0))), z > 0)
        else:
            target = 3 - z if i == 1 else 3 * (z // 2)
            relay = remote(own, own, zsnd.at[k, 1 + i], zrcv.at[k, zp], at_z(target))
            relay.wait_recv()
            send(relay, inner)
        send(remote(own, own, ysnd.at[k, i, 0], yrcv.at[k, i, 0], at_y(up)))
        send(remote(own, own, ysnd.at[k, i, 1], yrcv.at[k, i, 1], at_y(down)))

    def gather_y(k, i):
        zp = piece(i)
        for way, source, target, first in ((0, down, up, 0), (1, up, down, half)):
            whole = G.at[k, source, zp]
            remote(whole, whole, ysnd.at[k, i, way], yrcv.at[k, i, way], at_y(target)).wait_recv()
            part = G.at[k, source, zp, :, pl.ds(first, half)]
            send(remote(part, part, fsnd.at[k, i, way], frcv.at[k, i, way], at_y(target)))

    def gather_end(k):
        far = (y + 2) % NY
        for i in range(NZ):
            zp = piece(i)
            for way, first in ((0, 0), (1, half)):
                part = G.at[k, far, zp, :, pl.ds(first, half)]
                remote(part, part, fsnd.at[k, i, way], frcv.at[k, i, way], at_y(up)).wait_recv()

    def down_project(k):
        depth = ff // 4
        for n in range(4):
            g = G[k, :, :, :, n * depth:(n + 1) * depth].reshape(NY * NZ * ROWS, depth)
            part = jnp.dot(g, W[n * depth:(n + 1) * depth, :], preferred_element_type=F32)
            if n == 0:
                acc[...] = part
            elif n < 3:
                acc[...] += part
            else:
                Pb[k] = (acc[...] + part).astype(BF).reshape(NY, NZ, ROWS, feats)
        for j in range(1, ND):
            dd = (d + j) % ND
            send(remote(Pb.at[k, pl.ds(2 * (dd % 2), 2), dd // 2], R.at[k, j], dsnd.at[k, j], drcv.at[k, j], at_d(dd)))

    def boundary(k):
        total = res[:, k].astype(F32) + Pb[k, pl.ds(2 * (d % 2), 2), d // 2].astype(F32)
        for j in range(1, ND):
            remote(R.at[k, j], R.at[k, j], dsnd.at[k, j], drcv.at[k, j], at_d(d)).wait_recv()
        for j in range(1, ND):
            total = total + R[k, j].astype(F32)
        B[k] = total.astype(BF)
        send(remote(B.at[k], E.at[k, d // 2, d % 2], ssnd.at[k], srcv.at[k], ((s + 1) % NS, d, t)))

    def spread(k):
        own = E.at[k, d // 2, d % 2]
        remote(own, own, ssnd.at[k], srcv.at[k], at_d(d)).wait_recv()
        for j in range(1, ND):
            send(remote(own, own, gsnd.at[k, j], grcv.at[k, j], at_d((d + j) % ND)))

    def project(k):
        for j in range(1, ND):
            dd = (d + ND - j) % ND
            got = E.at[k, dd // 2, dd % 2]
            remote(got, got, gsnd.at[k, j], grcv.at[k, j], at_d(dd)).wait_recv()
        x = E[k].reshape(NY * NZ * ROWS, feats).astype(F32)
        scaled = (x * gain[...]).astype(BF)
        U[k] = jnp.dot(scaled, WP[...], preferred_element_type=F32).astype(BF).reshape(NZ, 2, 2, ROWS, 768)
        SQ[k] = lax.dot_general(
            jnp.ones((8, feats), BF), (x * x).astype(BF), (((1,), (1,)), ((), ())), preferred_element_type=F32
        )
        for j in range(1, NY):
            yy = (y + j) % NY
            send(remote(SQ.at[k], SY.at[k, j], qysnd.at[k, j], qyrcv.at[k, j], at_y(yy)))
            send(remote(U.at[k, :, yy // 2, yy % 2], RY.at[k, j], usnd.at[k, j], urcv.at[k, j], at_y(yy)))

    def sum_y(k):
        for j in range(1, NY):
            remote(SY.at[k, j], SY.at[k, j], qysnd.at[k, j], qyrcv.at[k, j], at_y(y)).wait_recv()
            remote(RY.at[k, j], RY.at[k, j], usnd.at[k, j], urcv.at[k, j], at_y(y)).wait_recv()
        total = U[k, :, y // 2, y % 2].astype(F32)
        squares = SQ[k]
        for j in range(1, NY):
            total = total + RY[k, j].astype(F32)
            squares = squares + SY[k, j]
        V[k] = total.astype(BF)
        SV[k] = squares
        for j in range(1, NZ):
            zz = (z + j) % NZ
            send(remote(SV.at[k], SZ.at[k, j], qzsnd.at[k, j], qzrcv.at[k, j], at_z(zz)))
            send(remote(V.at[k, zz], RZ.at[k, j], vsnd.at[k, j], vrcv.at[k, j], at_z(zz)))

    def sum_z(k):
        for j in range(1, NZ):
            remote(SZ.at[k, j], SZ.at[k, j], qzsnd.at[k, j], qzrcv.at[k, j], at_z(z)).wait_recv()
            remote(RZ.at[k, j], RZ.at[k, j], vsnd.at[k, j], vrcv.at[k, j], at_z(z)).wait_recv()
        total = V[k, z].astype(F32)
        squares = SV[k]
        for j in range(1, NZ):
            total = total + RZ[k, j].astype(F32)
            squares = squares + SZ[k, j]
        tokens = NY * NZ * ROWS
        lane = lax.broadcasted_iota(jnp.int32, (ROWS, tokens), 1)
        row = lax.broadcasted_iota(jnp.int32, (ROWS, tokens), 0)
        row_squares = jnp.broadcast_to(squares[0:1, :], (ROWS, tokens))
        own_squares = jnp.sum(jnp.where(lane == row + t * ROWS, row_squares, 0.0), axis=1, keepdims=True)
        values = total * lax.rsqrt(own_squares / D + EPSILON)
        cosine = ctab[k * ROWS:(k + 1) * ROWS, :]
        sine = stab[k * ROWS:(k + 1) * ROWS, :]

        def rotate(u):
            return (u * cosine + pltpu.roll(u, HD // 2, 1) * sine).astype(BF)

        for h in range(4):
            Qb[h, k * ROWS:(k + 1) * ROWS, :] = rotate(values[:, h * HD:(h + 1) * HD])
        KV[k, y, z, :, 0:HD] = rotate(values[:, 512:640])
        KV[k, y, z, :, HD:2 * HD] = values[:, 640:768].astype(BF)
        own = KV.at[k, y, z]
        for j in range(1, NZ):
            send(remote(own, own, kzsnd.at[k, j], kzrcv.at[k, j], at_z((z + j) % NZ)))

    def pairs_y(k):
        for j in range(1, NZ):
            got = KV.at[k, y, (z + NZ - j) % NZ]
            remote(got, got, kzsnd.at[k, j], kzrcv.at[k, j], at_z(z)).wait_recv()
        own = KV.at[k, y]
        for j in range(1, NY):
            send(remote(own, own, kysnd.at[k, j], kyrcv.at[k, j], at_y((y + j) % NY)))

    def pairs_end(k):
        for j in range(1, NY):
            got = KV.at[k, (y + NY - j) % NY]
            remote(got, got, kysnd.at[k, j], kyrcv.at[k, j], at_y(y)).wait_recv()

    def attend():
        tokens = NK * NY * NZ * ROWS
        queries = Qb[...].reshape(4 * 64, HD)
        keys = KV[:, :, :, :, 0:HD].reshape(tokens, HD)
        values = KV[:, :, :, :, HD:2 * HD].reshape(tokens, HD)
        scores = lax.dot_general(queries, keys, (((1,), (1,)), ((), ())), preferred_element_type=F32) * HD ** (-0.5)
        lane = lax.broadcasted_iota(jnp.int32, (1, tokens), 1)
        key_at = ((lane >> 4) & 3) * 256 + ((lane >> 6) & 3) * 64 + (lane >> 8) * 16 + (lane & 15)
        row = lax.broadcasted_iota(jnp.int32, (256, 1), 0)
        query_at = (row & 63) + t * 64
        scores = jnp.where(key_at <= query_at, scores, -1e30)
        weights = jnp.exp(scores - jnp.max(scores, axis=1, keepdims=True))
        share = (weights / jnp.sum(weights, axis=1, keepdims=True)).astype(BF)
        result = jnp.dot(share, values, preferred_element_type=F32).astype(BF)
        for h in range(4):
            out[:, h * HD:(h + 1) * HD] = result[h * 64:(h + 1) * 64, :]

    def step(f, k):
        if 0 <= k < NK:
            f(k)

    gather_z(0, 0)
    gather_z(1, 0)
    for i in range(1, NZ):
        gather_z(0, i)
    local[1].wait()
    local[2].wait()
    local[3].wait()
    for k in range(NK + 3):
        live = k < NK
        for i in range(NZ):
            if live:
                if i > 0 and k + 1 < NK:
                    gather_z(k + 1, i)
                if i == 0 and 0 < k and k + 1 < NK:
                    gather_z(k + 1, 0)
                gather_y(k, i)
            if i == 0:
                step(sum_y, k - 2)
            if i == 1:
                step(boundary, k - 1)
            if i == 2:
                step(sum_z, k - 2)
            if i == 3:
                step(spread, k - 1)
                step(pairs_y, k - 2)
        if live:
            gather_end(k)
            down_project(k)
        step(project, k - 1)
    for k in range(NK):
        pairs_end(k)
    attend()
    for cond, copy in sent:
        if cond is None:
            copy.wait_send()
        else:
            pl.when(cond)(copy.wait_send)


def per_device(hidden, down_weight, residual, norm_gain, query_weight, key_value_weight):
    own_rows, ff = hidden.shape[1:]
    feats = down_weight.shape[2]
    positions = (lax.axis_index("tensor") * own_rows + jnp.arange(own_rows, dtype=jnp.int32)).astype(F32)
    frequency = ROPE_BASE ** (-jnp.arange(HD // 2, dtype=F32) * 2.0 / HD)
    angles = positions[:, None] * frequency[None, :]
    cosine, sine = jnp.cos(angles), jnp.sin(angles)
    ctab = jnp.concatenate([cosine, cosine], axis=1)
    stab = jnp.concatenate([-sine, sine], axis=1)
    chunk = NY * NZ * ROWS
    dma = pltpu.SemaphoreType.DMA
    vmem = pl.BlockSpec(memory_space=pltpu.VMEM)
    hbm = pl.BlockSpec(memory_space=pl.ANY)
    attended = pl.pallas_call(
        kernel,
        out_shape=jax.ShapeDtypeStruct((own_rows, 512), BF),
        in_specs=[hbm, hbm, hbm, hbm, vmem, vmem, vmem, vmem],
        out_specs=vmem,
        scratch_shapes=[
            pltpu.VMEM((NK, NY, NZ, ROWS, ff), BF),
            pltpu.VMEM((ff, feats), BF),
            pltpu.VMEM((feats, 768), BF),
            pltpu.VMEM((chunk, feats), F32),
            pltpu.VMEM((NK, NY, NZ, ROWS, feats), BF),
            pltpu.VMEM((NK, ND, 2, ROWS, feats), BF),
            pltpu.VMEM((NK, 2, ROWS, feats), BF),
            pltpu.VMEM((NK, NZ, 2, 2, ROWS, feats), BF),
            pltpu.VMEM((NK, NZ, 2, 2, ROWS, 768), BF),
            pltpu.VMEM((NK, NY, NZ, ROWS, 768), BF),
            pltpu.VMEM((NK, NZ, ROWS, 768), BF),
            pltpu.VMEM((NK, NZ, ROWS, 768), BF),
            pltpu.VMEM((NK, 8, chunk), F32),
            pltpu.VMEM((NK, NY, 8, chunk), F32),
            pltpu.VMEM((NK, 8, chunk), F32),
            pltpu.VMEM((NK, NZ, 8, chunk), F32),
            pltpu.VMEM((4, own_rows, HD), BF),
            pltpu.VMEM((NK, NY, NZ, ROWS, 2 * HD), BF),
            dma((4,)),
            dma((NK, 5)), dma((NK, NZ)),
            dma((NK, NZ, 2)), dma((NK, NZ, 2)),
            dma((NK, NZ, 2)), dma((NK, NZ, 2)),
            dma((NK, ND)), dma((NK, ND)),
            dma((NK,)), dma((NK,)),
            dma((NK, ND)), dma((NK, ND)),
            dma((NK, NY)), dma((NK, NY)),
            dma((NK, NZ)), dma((NK, NZ)),
            dma((NK, NY)), dma((NK, NY)),
            dma((NK, NZ)), dma((NK, NZ)),
            dma((NK, NZ)), dma((NK, NZ)),
            dma((NK, NY)), dma((NK, NY)),
        ],
        compiler_params=pltpu.CompilerParams(collective_id=0, has_side_effects=True, vmem_limit_bytes=48 << 20),
    )(
        hidden.reshape(NK, ROWS, ff),
        down_weight[0],
        query_weight[0],
        key_value_weight[0],
        residual.reshape(2, NK, ROWS, feats),
        norm_gain,
        ctab,
        stab,
    )
    return attended[None]


def solution(mesh):
    placed = (
        P("section", "tensor", "dp"),
        P("section", "dp", "tensor"),
        P("section", "dp", "tensor"),
        P("section", "tensor"),
        P("section", "tensor", "dp"),
        P("section", "tensor", "dp"),
    )
    return jax.shard_map(
        per_device,
        mesh=mesh,
        in_specs=placed,
        out_specs=P("section", "tensor", "dp"),
        check_vma=False,
    )
```

```python
import jax
import jax.numpy as jnp
from jax import lax
from jax.experimental import pallas as pl
from jax.experimental.pallas import tpu as pltpu
from jax.sharding import PartitionSpec as P

D = 8192
HD = 128
ROPE_BASE = 500000.0
EPSILON = 1e-05

MESH = pl.DeviceIdType.MESH
NZ, NY, ND, NS = 4, 4, 8, 4
NK = 4
ROWS = 16
BF = jnp.bfloat16
F32 = jnp.float32


COLS = 22
ORDER = [
    ("ry", 1), ("ry", 0), ("gz", 0, 0), ("rf", 1), ("ry", 2), ("rf", 0), ("gz", 1, 0), ("gy", 0, 0),
    ("gz", 2, 0), ("ry", 3), ("rz", 0, 0), ("gz", 0, 1), ("rz", 1, 0), ("rf", 2), ("gz", 0, 2), ("rz", 0, 1),
    ("gz", 1, 1), ("rf", 3), ("gy", 1, 0), ("gz", 1, 2), ("gy", 0, 1), ("rz", 2, 0), ("gz", 0, 3), ("gy", 1, 1),
    ("gz", 2, 1), ("rz", 0, 2), ("gy", 2, 0), ("gz", 1, 3), ("gz", 2, 2), ("gy", 0, 2), ("rz", 3, 0), ("rz", 1, 1),
    ("rz", 1, 2), ("gy", 0, 3), ("gz", 2, 3), ("gz", 3, 0), ("rz", 0, 3), ("gy", 2, 1), ("ge", 0), ("rz", 2, 1),
    ("dp", 0), ("gy", 2, 2), ("rz", 1, 3), ("gy", 1, 2), ("gy", 1, 3), ("gy", 2, 3), ("rz", 3, 1), ("gy", 3, 0),
    ("rz", 3, 2), ("rz", 2, 2), ("gz", 3, 1), ("rz", 2, 3), ("bd", 0), ("ge", 1), ("dp", 1), ("gy", 3, 1),
    ("gz", 3, 2), ("ge", 2), ("gz", 3, 3), ("dp", 2), ("bd", 1), ("gy", 3, 2), ("gy", 3, 3), ("sp", 0),
    ("rz", 3, 3), ("sp", 1), ("bd", 2), ("ge", 3), ("dp", 3), ("pp", 0), ("pq", 0), ("sp", 2),
    ("pp", 1), ("bd", 3), ("pq", 1), ("ky", 0), ("pp", 2), ("sp", 3), ("kz", 0), ("pq", 2),
    ("ky", 1), ("qy", 0), ("ky", 2), ("pp", 3), ("pq", 3), ("qy", 2), ("py", 0), ("kz", 1),
    ("ky", 3), ("qy", 1), ("kz", 2), ("py", 1), ("qy", 3), ("kz", 3), ("py", 2), ("qz", 1),
    ("qz", 0), ("pe", 0), ("qz", 2), ("qz", 3), ("py", 3), ("pe", 2), ("pe", 1), ("at", 0, 2),
    ("at", 2, 3), ("pe", 3), ("at", 3, 4),
]
FLUSH = {("sp", 3): ("dp", 3), ("ky", 3): ("sp", 3), ("pe", 3): ("kz", 3)}


def kernel(
    hid, w_hbm, wq_hbm, wkv_hbm, res_hbm, gain_hbm, ctab_hbm, stab_hbm, out,
    res, gain, ctab, stab, peak, mass, mixed,
    G, W, WP, acc, Pb, R, B, E, XS, UK, UQ, RK, RQ, VK, VQ, ZK, ZQ, SQ, SY, SV, SZ, inv, Qb, KV,
    lsem, zsnd, zrcv, ysnd, yrcv, fsnd, frcv, bysnd, byrcv, bfsnd, bfrcv, bzsnd, bzrcv, dsnd, drcv, ssnd, srcv, gsnd, grcv,
    uksnd, ukrcv, uqsnd, uqrcv, vksnd, vkrcv, vqsnd, vqrcv, qysnd, qyrcv, qzsnd, qzrcv, kzsnd, kzrcv, kysnd, kyrcv,
):
    s = lax.axis_index("section")
    d = lax.axis_index("dp")
    t = lax.axis_index("tensor")
    z, y = t // NY, t % NY
    ff, feats = W.shape
    first_cols = ff * COLS // 28
    half = first_cols // 2
    rest = ff - first_cols
    near, later = pl.ds(0, first_cols), pl.ds(first_cols, rest)
    inner = jnp.logical_and(z > 0, z < NZ - 1)

    def at_z(zz):
        return (s, d, zz * NY + y)

    def at_y(yy):
        return (s, d, z * NY + yy)

    def at_d(dd):
        return (s, dd, t)

    def piece(i):
        return (z, z + 1 - 2 * (z % 2), 2 - z // 2, 3 - 3 * (z // 2))[i]

    def remote(src, dst, snd, rcv, where):
        return pltpu.make_async_remote_copy(
            src_ref=src, dst_ref=dst, send_sem=snd, recv_sem=rcv, device_id=where, device_id_type=MESH
        )

    sent = []

    def send(copy, cond=None):
        if cond is None:
            copy.start()
        else:
            pl.when(cond)(copy.start)
        sent.append((cond, copy))

    local = [
        pltpu.make_async_copy(hid, G.at[:, y, z], lsem.at[0]),
        pltpu.make_async_copy(w_hbm, W, lsem.at[1]),
        pltpu.make_async_copy(wq_hbm, WP.at[:, pl.ds(0, 512)], lsem.at[2]),
        pltpu.make_async_copy(wkv_hbm, WP.at[:, pl.ds(512, 256)], lsem.at[3]),
        pltpu.make_async_copy(res_hbm, res, lsem.at[4]),
        pltpu.make_async_copy(gain_hbm, gain, lsem.at[5]),
        pltpu.make_async_copy(ctab_hbm, ctab, lsem.at[6]),
        pltpu.make_async_copy(stab_hbm, stab, lsem.at[7]),
    ]
    for copy in local:
        copy.start()

    barrier = pltpu.get_barrier_semaphore()
    peers = [at_y((y + j) % NY) for j in range(1, NY)]
    peers += [at_z((z + j) % NZ) for j in range(1, NZ)]
    peers += [at_d((d + j) % ND) for j in range(1, ND)]
    peers += [((s + 1) % NS, d, t), ((s + NS - 1) % NS, d, t)]
    for peer in peers:
        pl.semaphore_signal(barrier, inc=1, device_id=peer, device_id_type=MESH)
    pl.semaphore_wait(barrier, len(peers))
    local[0].wait()

    up, down = (y + 1) % NY, (y + NY - 1) % NY

    def gather_z(k, i):
        zp = piece(i)
        own = G.at[k, y, zp, :, near]
        if i == 0:
            send(remote(own, own, zsnd.at[k, 0], zrcv.at[k, zp], at_z(jnp.minimum(z + 1, NZ - 1))), z < NZ - 1)
            send(remote(own, own, zsnd.at[k, 1], zrcv.at[k, zp], at_z(jnp.maximum(z - 1, 0))), z > 0)
        else:
            target = 3 - z if i == 1 else 3 * (z // 2)
            relay = remote(own, own, zsnd.at[k, 1 + i], zrcv.at[k, zp], at_z(target))
            relay.wait_recv()
            send(relay, inner)
        send(remote(own, own, ysnd.at[k, i, 0], yrcv.at[k, i, 0], at_y(up)))
        send(remote(own, own, ysnd.at[k, i, 1], yrcv.at[k, i, 1], at_y(down)))

    def gather_y(k, i):
        zp = piece(i)
        for way, source, target, first in ((0, down, up, 0), (1, up, down, half)):
            whole = G.at[k, source, zp, :, near]
            remote(whole, whole, ysnd.at[k, i, way], yrcv.at[k, i, way], at_y(target)).wait_recv()
            part = G.at[k, source, zp, :, pl.ds(first, half)]
            send(remote(part, part, fsnd.at[k, i, way], frcv.at[k, i, way], at_y(target)))

    def gather_end(k):
        far = (y + 2) % NY
        for i in range(NZ):
            zp = piece(i)
            for way, first in ((0, 0), (1, half)):
                part = G.at[k, far, zp, :, pl.ds(first, half)]
                remote(part, part, fsnd.at[k, i, way], frcv.at[k, i, way], at_y(up)).wait_recv()

    def rest_y(k):
        own = G.at[k, y, z, :, later]
        send(remote(own, own, bysnd.at[k, 0], byrcv.at[k, 0], at_y(up)))
        send(remote(own, own, bysnd.at[k, 1], byrcv.at[k, 1], at_y(down)))

    def rest_far(k):
        for way, source, target, first in ((0, down, up, 0), (1, up, down, rest // 2)):
            whole = G.at[k, source, z, :, later]
            remote(whole, whole, bysnd.at[k, way], byrcv.at[k, way], at_y(target)).wait_recv()
            part = G.at[k, source, z, :, pl.ds(first_cols + first, rest // 2)]
            send(remote(part, part, bfsnd.at[k, way], bfrcv.at[k, way], at_y(target)))

    def rest_z(k, i):
        zp = piece(i)
        own = G.at[k, :, zp, :, later]
        if i == 0:
            far = (y + 2) % NY
            for way, first in ((0, 0), (1, rest // 2)):
                part = G.at[k, far, z, :, pl.ds(first_cols + first, rest // 2)]
                remote(part, part, bfsnd.at[k, way], bfrcv.at[k, way], at_y(up)).wait_recv()
            send(remote(own, own, bzsnd.at[k, 0], bzrcv.at[k, zp], at_z(jnp.minimum(z + 1, NZ - 1))), z < NZ - 1)
            send(remote(own, own, bzsnd.at[k, 1], bzrcv.at[k, zp], at_z(jnp.maximum(z - 1, 0))), z > 0)
        else:
            target = 3 - z if i == 1 else 3 * (z // 2)
            relay = remote(own, own, bzsnd.at[k, 1 + i], bzrcv.at[k, zp], at_z(target))
            relay.wait_recv()
            send(relay, inner)

    def down_project(k):
        depth = ff // 4
        for n in range(4):
            g = G[k, :, :, :, n * depth:(n + 1) * depth].reshape(NY * NZ * ROWS, depth)
            part = jnp.dot(g, W[n * depth:(n + 1) * depth, :], preferred_element_type=F32)
            if n == 0:
                acc[...] = part
            elif n < 3:
                acc[...] += part
            else:
                Pb[k] = (acc[...] + part).astype(BF).reshape(NY, NZ, ROWS, feats)
        for j in range(1, ND):
            dd = (d + j) % ND
            send(remote(Pb.at[k, pl.ds(2 * (dd % 2), 2), dd // 2], R.at[k, j], dsnd.at[k, j], drcv.at[k, j], at_d(dd)))

    def boundary(k):
        total = res[:, k].astype(F32) + Pb[k, pl.ds(2 * (d % 2), 2), d // 2].astype(F32)
        for j in range(1, ND):
            remote(R.at[k, j], R.at[k, j], dsnd.at[k, j], drcv.at[k, j], at_d(d)).wait_recv()
        for j in range(1, ND):
            total = total + R[k, j].astype(F32)
        B[k] = total.astype(BF)
        send(remote(B.at[k], E.at[k, d // 2, d % 2], ssnd.at[k], srcv.at[k], ((s + 1) % NS, d, t)))

    def spread(k):
        own = E.at[k, d // 2, d % 2]
        remote(own, own, ssnd.at[k], srcv.at[k], at_d(d)).wait_recv()
        for j in range(1, ND):
            send(remote(own, own, gsnd.at[k, j], grcv.at[k, j], at_d((d + j) % ND)))

    def project_pairs(k):
        for j in range(1, ND):
            dd = (d + ND - j) % ND
            got = E.at[k, dd // 2, dd % 2]
            remote(got, got, gsnd.at[k, j], grcv.at[k, j], at_d(dd)).wait_recv()
        x = E[k].reshape(NY * NZ * ROWS, feats).astype(F32)
        scaled = (x * gain[...]).astype(BF)
        XS[k] = scaled
        UK[k] = jnp.dot(scaled, WP[:, 512:768], preferred_element_type=F32).astype(BF).reshape(NZ, 2, 2, ROWS, 256)
        SQ[k] = lax.dot_general(
            jnp.ones((8, feats), BF), (x * x).astype(BF), (((1,), (1,)), ((), ())), preferred_element_type=F32
        )
        for j in range(1, NY):
            yy = (y + j) % NY
            send(remote(UK.at[k, :, yy // 2, yy % 2], RK.at[k, j], uksnd.at[k, j], ukrcv.at[k, j], at_y(yy)))
            send(remote(SQ.at[k], SY.at[k, j], qysnd.at[k, j], qyrcv.at[k, j], at_y(yy)))

    def project_queries(k):
        UQ[k] = jnp.dot(XS[k], WP[:, 0:512], preferred_element_type=F32).astype(BF).reshape(NZ, 2, 2, ROWS, 512)
        for j in range(1, NY):
            yy = (y + j) % NY
            send(remote(UQ.at[k, :, yy // 2, yy % 2], RQ.at[k, j], uqsnd.at[k, j], uqrcv.at[k, j], at_y(yy)))

    def sum_pairs_y(k):
        for j in range(1, NY):
            remote(RK.at[k, j], RK.at[k, j], uksnd.at[k, j], ukrcv.at[k, j], at_y(y)).wait_recv()
            remote(SY.at[k, j], SY.at[k, j], qysnd.at[k, j], qyrcv.at[k, j], at_y(y)).wait_recv()
        total = UK[k, :, y // 2, y % 2].astype(F32)
        squares = SQ[k]
        for j in range(1, NY):
            total = total + RK[k, j].astype(F32)
            squares = squares + SY[k, j]
        VK[k] = total.astype(BF)
        SV[k] = squares
        for j in range(1, NZ):
            zz = (z + j) % NZ
            send(remote(VK.at[k, zz], ZK.at[k, j], vksnd.at[k, j], vkrcv.at[k, j], at_z(zz)))
            send(remote(SV.at[k], SZ.at[k, j], qzsnd.at[k, j], qzrcv.at[k, j], at_z(zz)))

    def sum_queries_y(k):
        for j in range(1, NY):
            remote(RQ.at[k, j], RQ.at[k, j], uqsnd.at[k, j], uqrcv.at[k, j], at_y(y)).wait_recv()
        total = UQ[k, :, y // 2, y % 2].astype(F32)
        for j in range(1, NY):
            total = total + RQ[k, j].astype(F32)
        VQ[k] = total.astype(BF)
        for j in range(1, NZ):
            zz = (z + j) % NZ
            send(remote(VQ.at[k, zz], ZQ.at[k, j], vqsnd.at[k, j], vqrcv.at[k, j], at_z(zz)))

    def rotate(u, k):
        rows = pl.ds(k * ROWS, ROWS)
        return (u * ctab[rows, :] + pltpu.roll(u, HD // 2, 1) * stab[rows, :]).astype(BF)

    def sum_pairs_z(k):
        for j in range(1, NZ):
            remote(ZK.at[k, j], ZK.at[k, j], vksnd.at[k, j], vkrcv.at[k, j], at_z(z)).wait_recv()
            remote(SZ.at[k, j], SZ.at[k, j], qzsnd.at[k, j], qzrcv.at[k, j], at_z(z)).wait_recv()
        total = VK[k, z].astype(F32)
        squares = SV[k]
        for j in range(1, NZ):
            total = total + ZK[k, j].astype(F32)
            squares = squares + SZ[k, j]
        tokens = NY * NZ * ROWS
        lane = lax.broadcasted_iota(jnp.int32, (ROWS, tokens), 1)
        row = lax.broadcasted_iota(jnp.int32, (ROWS, tokens), 0)
        row_squares = jnp.broadcast_to(squares[0:1, :], (ROWS, tokens))
        own_squares = jnp.sum(jnp.where(lane == row + t * ROWS, row_squares, 0.0), axis=1, keepdims=True)
        inverse = lax.rsqrt(own_squares / D + EPSILON)
        inv[k] = jnp.broadcast_to(inverse, (ROWS, HD))
        KV[k, y, z, :, 0:HD] = rotate(total[:, 0:HD] * inverse, k)
        KV[k, y, z, :, HD:2 * HD] = (total[:, HD:2 * HD] * inverse).astype(BF)
        own = KV.at[k, y, z]
        for j in range(1, NZ):
            send(remote(own, own, kzsnd.at[k, j], kzrcv.at[k, j], at_z((z + j) % NZ)))

    def sum_queries_z(k):
        for j in range(1, NZ):
            remote(ZQ.at[k, j], ZQ.at[k, j], vqsnd.at[k, j], vqrcv.at[k, j], at_z(z)).wait_recv()
        total = VQ[k, z].astype(F32)
        for j in range(1, NZ):
            total = total + ZQ[k, j].astype(F32)
        for h in range(4):
            Qb[h, k * ROWS:(k + 1) * ROWS, :] = rotate(total[:, h * HD:(h + 1) * HD] * inv[k], k)

    def pairs_y(k):
        for j in range(1, NZ):
            got = KV.at[k, y, (z + NZ - j) % NZ]
            remote(got, got, kzsnd.at[k, j], kzrcv.at[k, j], at_z(z)).wait_recv()
        own = KV.at[k, y]
        for j in range(1, NY):
            send(remote(own, own, kysnd.at[k, j], kyrcv.at[k, j], at_y((y + j) % NY)))

    def pairs_end(k):
        for j in range(1, NY):
            got = KV.at[k, (y + NY - j) % NY]
            remote(got, got, kysnd.at[k, j], kyrcv.at[k, j], at_y(y)).wait_recv()

    def attend(first, last):
        tokens = (last - first) * NY * NZ * ROWS
        queries = Qb[...].reshape(4 * 64, HD)
        keys = KV[first:last, :, :, :, 0:HD].reshape(tokens, HD)
        values = KV[first:last, :, :, :, HD:2 * HD].reshape(tokens, HD)
        scores = lax.dot_general(queries, keys, (((1,), (1,)), ((), ())), preferred_element_type=F32) * HD ** (-0.5)
        lane = lax.broadcasted_iota(jnp.int32, (1, tokens), 1) + first * NY * NZ * ROWS
        key_at = ((lane >> 4) & 3) * 256 + ((lane >> 6) & 3) * 64 + (lane >> 8) * 16 + (lane & 15)
        row = lax.broadcasted_iota(jnp.int32, (256, 1), 0)
        query_at = (row & 63) + t * 64
        scores = jnp.where(key_at <= query_at, scores, -1e30)
        top = jnp.max(scores, axis=1, keepdims=True)
        if first > 0:
            top = jnp.maximum(top, peak[...])
        weights = jnp.exp(scores - top)
        total = jnp.sum(weights, axis=1, keepdims=True)
        result = jnp.dot(weights.astype(BF), values, preferred_element_type=F32)
        if first > 0:
            fade = jnp.exp(peak[...] - top)
            total = total + mass[...] * fade
            result = result + mixed[...] * fade
        if last < NK:
            peak[...] = top
            mass[...] = total
            mixed[...] = result
        else:
            result = (result / total).astype(BF)
            for h in range(4):
                out[:, h * HD:(h + 1) * HD] = result[h * 64:(h + 1) * 64, :]

    def flush(count):
        for cond, copy in sent[:count]:
            if cond is None:
                copy.wait_send()
            else:
                pl.when(cond)(copy.wait_send)
        del sent[:count]

    steps = dict(
        gz=gather_z, gy=gather_y, ge=gather_end, ry=rest_y, rf=rest_far, rz=rest_z, dp=down_project, bd=boundary,
        sp=spread, pp=project_pairs, pq=project_queries, ky=sum_pairs_y, qy=sum_queries_y, kz=sum_pairs_z,
        qz=sum_queries_z, py=pairs_y, pe=pairs_end, at=attend,
    )
    waited = False
    marks = {}
    for name, *at in ORDER:
        token = (name, *at)
        if name == "dp" and not waited:
            waited = True
            for copy in local[1:]:
                copy.wait()
        if token in FLUSH:
            count = marks[FLUSH[token]] - marks.get("done", 0)
            marks["done"] = marks[FLUSH[token]]
            flush(count)
        marks[token] = marks.get("done", 0) + len(sent)
        steps[name](*at)
    flush(len(sent))


def per_device(hidden, down_weight, residual, norm_gain, query_weight, key_value_weight):
    own_rows, ff = hidden.shape[1:]
    feats = down_weight.shape[2]
    positions = (lax.axis_index("tensor") * own_rows + jnp.arange(own_rows, dtype=jnp.int32)).astype(F32)
    frequency = ROPE_BASE ** (-jnp.arange(HD // 2, dtype=F32) * 2.0 / HD)
    angles = positions[:, None] * frequency[None, :]
    cosine, sine = jnp.cos(angles), jnp.sin(angles)
    ctab = jnp.concatenate([cosine, cosine], axis=1)
    stab = jnp.concatenate([-sine, sine], axis=1)
    chunk = NY * NZ * ROWS
    dma = pltpu.SemaphoreType.DMA
    vmem = pl.BlockSpec(memory_space=pltpu.VMEM)
    hbm = pl.BlockSpec(memory_space=pltpu.HBM)
    attended = pl.pallas_call(
        kernel,
        out_shape=jax.ShapeDtypeStruct((own_rows, 512), BF),
        in_specs=[hbm] * 8,
        out_specs=vmem,
        scratch_shapes=[
            pltpu.VMEM((2, NK, ROWS, feats), BF),
            pltpu.VMEM((1, feats), F32),
            pltpu.VMEM((own_rows, HD), F32),
            pltpu.VMEM((own_rows, HD), F32),
            pltpu.VMEM((4 * own_rows, 1), F32),
            pltpu.VMEM((4 * own_rows, 1), F32),
            pltpu.VMEM((4 * own_rows, HD), F32),
            pltpu.VMEM((NK, NY, NZ, ROWS, ff), BF),
            pltpu.VMEM((ff, feats), BF),
            pltpu.VMEM((feats, 768), BF),
            pltpu.VMEM((chunk, feats), F32),
            pltpu.VMEM((NK, NY, NZ, ROWS, feats), BF),
            pltpu.VMEM((NK, ND, 2, ROWS, feats), BF),
            pltpu.VMEM((NK, 2, ROWS, feats), BF),
            pltpu.VMEM((NK, NZ, 2, 2, ROWS, feats), BF),
            pltpu.VMEM((NK, chunk, feats), BF),
            pltpu.VMEM((NK, NZ, 2, 2, ROWS, 256), BF),
            pltpu.VMEM((NK, NZ, 2, 2, ROWS, 512), BF),
            pltpu.VMEM((NK, NY, NZ, ROWS, 256), BF),
            pltpu.VMEM((NK, NY, NZ, ROWS, 512), BF),
            pltpu.VMEM((NK, NZ, ROWS, 256), BF),
            pltpu.VMEM((NK, NZ, ROWS, 512), BF),
            pltpu.VMEM((NK, NZ, ROWS, 256), BF),
            pltpu.VMEM((NK, NZ, ROWS, 512), BF),
            pltpu.VMEM((NK, 8, chunk), F32),
            pltpu.VMEM((NK, NY, 8, chunk), F32),
            pltpu.VMEM((NK, 8, chunk), F32),
            pltpu.VMEM((NK, NZ, 8, chunk), F32),
            pltpu.VMEM((NK, ROWS, HD), F32),
            pltpu.VMEM((4, own_rows, HD), BF),
            pltpu.VMEM((NK, NY, NZ, ROWS, 2 * HD), BF),
            dma((8,)),
            dma((NK, 5)), dma((NK, NZ)),
            dma((NK, NZ, 2)), dma((NK, NZ, 2)),
            dma((NK, NZ, 2)), dma((NK, NZ, 2)),
            dma((NK, 2)), dma((NK, 2)),
            dma((NK, 2)), dma((NK, 2)),
            dma((NK, 5)), dma((NK, NZ)),
            dma((NK, ND)), dma((NK, ND)),
            dma((NK,)), dma((NK,)),
            dma((NK, ND)), dma((NK, ND)),
            dma((NK, NY)), dma((NK, NY)),
            dma((NK, NY)), dma((NK, NY)),
            dma((NK, NZ)), dma((NK, NZ)),
            dma((NK, NZ)), dma((NK, NZ)),
            dma((NK, NY)), dma((NK, NY)),
            dma((NK, NZ)), dma((NK, NZ)),
            dma((NK, NZ)), dma((NK, NZ)),
            dma((NK, NY)), dma((NK, NY)),
        ],
        compiler_params=pltpu.CompilerParams(collective_id=0, has_side_effects=True, vmem_limit_bytes=62 << 20),
    )(
        hidden.reshape(NK, ROWS, ff),
        down_weight[0],
        query_weight[0],
        key_value_weight[0],
        residual.reshape(2, NK, ROWS, feats),
        norm_gain,
        ctab,
        stab,
    )
    return attended[None]


def solution(mesh):
    placed = (
        P("section", "tensor", "dp"),
        P("section", "dp", "tensor"),
        P("section", "dp", "tensor"),
        P("section", "tensor"),
        P("section", "tensor", "dp"),
        P("section", "tensor", "dp"),
    )
    return jax.shard_map(
        per_device,
        mesh=mesh,
        in_specs=placed,
        out_specs=P("section", "tensor", "dp"),
        check_vma=False,
    )
```

```python
import jax
import jax.numpy as jnp
from jax import lax
from jax.experimental import pallas as pl
from jax.experimental.pallas import tpu as pltpu
from jax.sharding import PartitionSpec as P

D = 8192
HD = 128
ROPE_BASE = 500000.0
EPSILON = 1e-05

MESH = pl.DeviceIdType.MESH
NZ, NY, ND, NS = 4, 4, 8, 4
NK = 4
ROWS = 16
BF = jnp.bfloat16
F32 = jnp.float32


COLS = 24
ORDER = [
    ("ry", 1), ("ry", 0), ("ry", 3), ("gz", 0, 0), ("gz", 1, 0), ("rf", 3), ("rf", 1), ("rf", 0),
    ("ry", 2), ("gz", 0, 1), ("gz", 1, 1), ("gz", 2, 0), ("gz", 0, 2), ("rz", 1, 0), ("rz", 0, 0), ("gy", 0, 0),
    ("rf", 2), ("gz", 0, 3), ("gy", 2, 0), ("gz", 2, 1), ("gy", 0, 1), ("rz", 1, 1), ("gz", 1, 2), ("gy", 0, 2),
    ("rz", 2, 0), ("gy", 1, 0), ("gz", 1, 3), ("rz", 0, 1), ("gy", 0, 3), ("rz", 0, 2), ("rz", 3, 0), ("gz", 3, 0),
    ("gz", 2, 2), ("rz", 0, 3), ("gz", 2, 3), ("rz", 1, 2), ("rz", 2, 1), ("gy", 1, 1), ("rz", 1, 3), ("ge", 0),
    ("dp", 0), ("gy", 1, 2), ("rz", 2, 2), ("gy", 1, 3), ("rz", 3, 1), ("gy", 2, 1), ("gz", 3, 1), ("rz", 3, 2),
    ("gy", 2, 2), ("bd", 0), ("gy", 2, 3), ("gz", 3, 2), ("ge", 1), ("rz", 2, 3), ("dp", 1), ("gy", 3, 0),
    ("gz", 3, 3), ("sp", 0), ("gy", 3, 1), ("ge", 2), ("bd", 1), ("dp", 2), ("rz", 3, 3), ("gy", 3, 2),
    ("gy", 3, 3), ("sp", 1), ("bd", 2), ("ge", 3), ("dp", 3), ("pp", 0), ("pq", 0), ("sp", 2),
    ("pp", 1), ("pq", 1), ("bd", 3), ("pp", 2), ("pq", 2), ("sp", 3), ("ky", 1), ("ky", 0),
    ("qy", 1), ("pp", 3), ("ky", 2), ("pq", 3), ("kz", 0), ("qy", 0), ("ky", 3), ("kz", 2),
    ("kz", 1), ("py", 0), ("qy", 2), ("qz", 0), ("qz", 1), ("kz", 3), ("py", 2), ("qy", 3),
    ("py", 1), ("py", 3), ("qz", 2), ("pe", 2), ("pe", 0), ("pe", 1), ("qz", 3), ("at", 0, 2),
    ("at", 2, 3), ("pe", 3), ("at", 3, 4),
]
LOADED = min(ORDER.index(("dp", k)) for k in range(NK))
GATHERED = ORDER.index(("sp", 3))
LEFT = ORDER.index(("at", 3, 4)) - 1


def kernel(
    hid, w_hbm, wq_hbm, wkv_hbm, res_hbm, gain_hbm, ctab_hbm, stab_hbm, out,
    res, gain, ctab, stab, peak, mass, mixed,
    G, W, WP, acc, Pb, R, B, E, XS, UK, UQ, RK, RQ, VK, VQ, ZK, ZQ, SQ, SY, SV, SZ, inv, Qb, KV,
    lsem, zsnd, osnd,
    zrcv, yrcv, frcv, byrcv, bfrcv, bzrcv,
    drcv, srcv, grcv, ukrcv, uqrcv, vkrcv,
    vqrcv, qyrcv, qzrcv, kzrcv, kyrcv,
):
    s = lax.axis_index("section")
    d = lax.axis_index("dp")
    t = lax.axis_index("tensor")
    z, y = t // NY, t % NY
    ff, feats = W.shape
    first_cols = ff * COLS // 28
    half = first_cols // 2
    rest = ff - first_cols
    near, later = pl.ds(0, first_cols), pl.ds(first_cols, rest)
    inner = jnp.logical_and(z > 0, z < NZ - 1)

    def at_z(zz):
        return (s, d, zz * NY + y)

    def at_y(yy):
        return (s, d, z * NY + yy)

    def at_d(dd):
        return (s, dd, t)

    def piece(i):
        return (z, z + 1 - 2 * (z % 2), 2 - z // 2, 3 - 3 * (z // 2))[i]

    def remote(src, dst, snd, rcv, where):
        return pltpu.make_async_remote_copy(
            src_ref=src, dst_ref=dst, send_sem=snd, recv_sem=rcv, device_id=where, device_id_type=MESH
        )

    def send(copy, cond=None):
        if cond is None:
            copy.start()
        else:
            pl.when(cond)(copy.start)

    def drain(ref, sem):
        pltpu.make_async_copy(ref, ref, sem).wait()

    local = [
        pltpu.make_async_copy(hid, G.at[:, y, z], lsem.at[0]),
        pltpu.make_async_copy(w_hbm, W, lsem.at[1]),
        pltpu.make_async_copy(wq_hbm, WP.at[:, pl.ds(0, 512)], lsem.at[2]),
        pltpu.make_async_copy(wkv_hbm, WP.at[:, pl.ds(512, 256)], lsem.at[3]),
        pltpu.make_async_copy(res_hbm, res, lsem.at[4]),
        pltpu.make_async_copy(gain_hbm, gain, lsem.at[5]),
        pltpu.make_async_copy(ctab_hbm, ctab, lsem.at[6]),
        pltpu.make_async_copy(stab_hbm, stab, lsem.at[7]),
    ]
    for copy in local:
        copy.start()

    barrier = pltpu.get_barrier_semaphore()
    peers = [at_y((y + j) % NY) for j in range(1, NY)]
    peers += [at_z((z + j) % NZ) for j in range(1, NZ)]
    peers += [at_d((d + j) % ND) for j in range(1, ND)]
    peers += [((s + 1) % NS, d, t), ((s + NS - 1) % NS, d, t)]
    for peer in peers:
        pl.semaphore_signal(barrier, inc=1, device_id=peer, device_id_type=MESH)
    pl.semaphore_wait(barrier, len(peers))
    local[0].wait()

    up, down = (y + 1) % NY, (y + NY - 1) % NY

    def gather_z(k, i):
        zp = piece(i)
        own = G.at[k, y, zp, :, near]
        if i == 0:
            send(remote(own, own, zsnd.at[0], zrcv.at[k, zp], at_z(jnp.minimum(z + 1, NZ - 1))), z < NZ - 1)
            send(remote(own, own, zsnd.at[0], zrcv.at[k, zp], at_z(jnp.maximum(z - 1, 0))), z > 0)
        else:
            target = 3 - z if i == 1 else 3 * (z // 2)
            relay = remote(own, own, zsnd.at[1], zrcv.at[k, zp], at_z(target))
            relay.wait_recv()
            send(relay, inner)
        send(remote(own, own, osnd.at[0], yrcv.at[k, i, 0], at_y(up)))
        send(remote(own, own, osnd.at[0], yrcv.at[k, i, 1], at_y(down)))

    def gather_y(k, i):
        zp = piece(i)
        for way, source, target, first in ((0, down, up, 0), (1, up, down, half)):
            whole = G.at[k, source, zp, :, near]
            drain(whole, yrcv.at[k, i, way])
            part = G.at[k, source, zp, :, pl.ds(first, half)]
            send(remote(part, part, osnd.at[1], frcv.at[k], at_y(target)))

    def gather_end(k):
        drain(G.at[k, (y + 2) % NY, :, :, near], frcv.at[k])

    def rest_y(k):
        own = G.at[k, y, z, :, later]
        send(remote(own, own, osnd.at[2], byrcv.at[k, 0], at_y(up)))
        send(remote(own, own, osnd.at[2], byrcv.at[k, 1], at_y(down)))

    def rest_far(k):
        for way, source, target, first in ((0, down, up, 0), (1, up, down, rest // 2)):
            whole = G.at[k, source, z, :, later]
            drain(whole, byrcv.at[k, way])
            part = G.at[k, source, z, :, pl.ds(first_cols + first, rest // 2)]
            send(remote(part, part, osnd.at[3], bfrcv.at[k], at_y(target)))

    def rest_z(k, i):
        zp = piece(i)
        own = G.at[k, :, zp, :, later]
        if i == 0:
            drain(G.at[k, (y + 2) % NY, z, :, later], bfrcv.at[k])
            send(remote(own, own, zsnd.at[2], bzrcv.at[k, zp], at_z(jnp.minimum(z + 1, NZ - 1))), z < NZ - 1)
            send(remote(own, own, zsnd.at[2], bzrcv.at[k, zp], at_z(jnp.maximum(z - 1, 0))), z > 0)
        else:
            target = 3 - z if i == 1 else 3 * (z // 2)
            relay = remote(own, own, zsnd.at[3], bzrcv.at[k, zp], at_z(target))
            relay.wait_recv()
            send(relay, inner)

    def down_project(k):
        depth = ff // 4
        for n in range(4):
            g = G[k, :, :, :, n * depth:(n + 1) * depth].reshape(NY * NZ * ROWS, depth)
            part = jnp.dot(g, W[n * depth:(n + 1) * depth, :], preferred_element_type=F32)
            if n == 0:
                acc[...] = part
            elif n < 3:
                acc[...] += part
            else:
                Pb[k] = (acc[...] + part).astype(BF).reshape(NY, NZ, ROWS, feats)
        for j in range(1, ND):
            dd = (d + j) % ND
            send(remote(Pb.at[k, pl.ds(2 * (dd % 2), 2), dd // 2], R.at[k, j - 1], osnd.at[4], drcv.at[k], at_d(dd)))

    def boundary(k):
        total = res[:, k].astype(F32) + Pb[k, pl.ds(2 * (d % 2), 2), d // 2].astype(F32)
        drain(R.at[k], drcv.at[k])
        for j in range(ND - 1):
            total = total + R[k, j].astype(F32)
        B[k] = total.astype(BF)
        send(remote(B.at[k], E.at[k, d // 2, d % 2], osnd.at[5], srcv.at[k], ((s + 1) % NS, d, t)))

    def spread(k):
        own = E.at[k, d // 2, d % 2]
        drain(own, srcv.at[k])
        for j in range(1, ND):
            send(remote(own, own, osnd.at[6], grcv.at[k], at_d((d + j) % ND)))

    def project_pairs(k):
        drain(R.at[k], grcv.at[k])
        x = E[k].reshape(NY * NZ * ROWS, feats).astype(F32)
        scaled = (x * gain[...]).astype(BF)
        XS[k] = scaled
        UK[k] = jnp.dot(scaled, WP[:, 512:768], preferred_element_type=F32).astype(BF).reshape(NZ, 2, 2, ROWS, 256)
        SQ[k] = lax.dot_general(
            jnp.ones((8, feats), BF), (x * x).astype(BF), (((1,), (1,)), ((), ())), preferred_element_type=F32
        )
        for j in range(1, NY):
            yy = (y + j) % NY
            send(remote(UK.at[k, :, yy // 2, yy % 2], RK.at[k, j - 1], osnd.at[7], ukrcv.at[k], at_y(yy)))
            send(remote(SQ.at[k], SY.at[k, j - 1], osnd.at[8], qyrcv.at[k], at_y(yy)))

    def project_queries(k):
        UQ[k] = jnp.dot(XS[k], WP[:, 0:512], preferred_element_type=F32).astype(BF).reshape(NZ, 2, 2, ROWS, 512)
        for j in range(1, NY):
            yy = (y + j) % NY
            send(remote(UQ.at[k, :, yy // 2, yy % 2], RQ.at[k, j - 1], osnd.at[9], uqrcv.at[k], at_y(yy)))

    def sum_pairs_y(k):
        drain(RK.at[k], ukrcv.at[k])
        drain(SY.at[k], qyrcv.at[k])
        total = UK[k, :, y // 2, y % 2].astype(F32)
        squares = SQ[k]
        for j in range(1, NY):
            total = total + RK[k, j - 1].astype(F32)
            squares = squares + SY[k, j - 1]
        VK[k] = total.astype(BF)
        SV[k] = squares
        for j in range(1, NZ):
            zz = (z + j) % NZ
            send(remote(VK.at[k, zz], ZK.at[k, j - 1], osnd.at[10], vkrcv.at[k], at_z(zz)))
            send(remote(SV.at[k], SZ.at[k, j - 1], osnd.at[11], qzrcv.at[k], at_z(zz)))

    def sum_queries_y(k):
        drain(RQ.at[k], uqrcv.at[k])
        total = UQ[k, :, y // 2, y % 2].astype(F32)
        for j in range(1, NY):
            total = total + RQ[k, j - 1].astype(F32)
        VQ[k] = total.astype(BF)
        for j in range(1, NZ):
            zz = (z + j) % NZ
            send(remote(VQ.at[k, zz], ZQ.at[k, j - 1], osnd.at[12], vqrcv.at[k], at_z(zz)))

    def rotate(u, k):
        rows = pl.ds(k * ROWS, ROWS)
        return (u * ctab[rows, :] + pltpu.roll(u, HD // 2, 1) * stab[rows, :]).astype(BF)

    def sum_pairs_z(k):
        drain(ZK.at[k], vkrcv.at[k])
        drain(SZ.at[k], qzrcv.at[k])
        total = VK[k, z].astype(F32)
        squares = SV[k]
        for j in range(1, NZ):
            total = total + ZK[k, j - 1].astype(F32)
            squares = squares + SZ[k, j - 1]
        tokens = NY * NZ * ROWS
        lane = lax.broadcasted_iota(jnp.int32, (ROWS, tokens), 1)
        row = lax.broadcasted_iota(jnp.int32, (ROWS, tokens), 0)
        row_squares = jnp.broadcast_to(squares[0:1, :], (ROWS, tokens))
        own_squares = jnp.sum(jnp.where(lane == row + t * ROWS, row_squares, 0.0), axis=1, keepdims=True)
        inverse = lax.rsqrt(own_squares / D + EPSILON)
        inv[k] = jnp.broadcast_to(inverse, (ROWS, HD))
        KV[k, y, z, :, 0:HD] = rotate(total[:, 0:HD] * inverse, k)
        KV[k, y, z, :, HD:2 * HD] = (total[:, HD:2 * HD] * inverse).astype(BF)
        own = KV.at[k, y, z]
        for j in range(1, NZ):
            send(remote(own, own, osnd.at[13], kzrcv.at[k], at_z((z + j) % NZ)))

    def sum_queries_z(k):
        drain(ZQ.at[k], vqrcv.at[k])
        total = VQ[k, z].astype(F32)
        for j in range(1, NZ):
            total = total + ZQ[k, j - 1].astype(F32)
        for h in range(4):
            Qb[h, k * ROWS:(k + 1) * ROWS, :] = rotate(total[:, h * HD:(h + 1) * HD] * inv[k], k)

    def pairs_y(k):
        drain(KV.at[k, y, pl.ds(0, NZ - 1)], kzrcv.at[k])
        own = KV.at[k, y]
        for j in range(1, NY):
            send(remote(own, own, osnd.at[14], kyrcv.at[k], at_y((y + j) % NY)))

    def pairs_end(k):
        drain(KV.at[k, pl.ds(0, NY - 1)], kyrcv.at[k])

    def attend(first, last):
        tokens = (last - first) * NY * NZ * ROWS
        queries = Qb[...].reshape(4 * 64, HD)
        keys = KV[first:last, :, :, :, 0:HD].reshape(tokens, HD)
        values = KV[first:last, :, :, :, HD:2 * HD].reshape(tokens, HD)
        scores = lax.dot_general(queries, keys, (((1,), (1,)), ((), ())), preferred_element_type=F32) * HD ** (-0.5)
        lane = lax.broadcasted_iota(jnp.int32, (1, tokens), 1) + first * NY * NZ * ROWS
        key_at = ((lane >> 4) & 3) * 256 + ((lane >> 6) & 3) * 64 + (lane >> 8) * 16 + (lane & 15)
        row = lax.broadcasted_iota(jnp.int32, (256, 1), 0)
        query_at = (row & 63) + t * 64
        scores = jnp.where(key_at <= query_at, scores, -1e30)
        top = jnp.max(scores, axis=1, keepdims=True)
        if first > 0:
            top = jnp.maximum(top, peak[...])
        weights = jnp.exp(scores - top)
        total = jnp.sum(weights, axis=1, keepdims=True)
        result = jnp.dot(weights.astype(BF), values, preferred_element_type=F32)
        if first > 0:
            fade = jnp.exp(peak[...] - top)
            total = total + mass[...] * fade
            result = result + mixed[...] * fade
        if last < NK:
            peak[...] = top
            mass[...] = total
            mixed[...] = result
        else:
            result = (result / total).astype(BF)
            for h in range(4):
                out[:, h * HD:(h + 1) * HD] = result[h * 64:(h + 1) * 64, :]

    def gathered():
        @pl.when(inner)
        def _():
            drain(G.at[:, 0, pl.ds(0, 2), :, near], zsnd.at[0])
            drain(G.at[:, 0, pl.ds(0, 3), :, near], zsnd.at[1])
            drain(G.at[:, pl.ds(0, 2), :, :, later], zsnd.at[2])
            drain(G.at[:, pl.ds(0, 3), :, :, later], zsnd.at[3])

        @pl.when(jnp.logical_not(inner))
        def _():
            drain(G.at[:, 0, 0, :, near], zsnd.at[0])
            drain(G.at[:, 0, :, :, later], zsnd.at[2])

        drain(G.at[:, pl.ds(0, 2), :, :, near], osnd.at[0])
        drain(G.at[:, 0, :, :, near], osnd.at[1])
        drain(G.at[:, 0, pl.ds(0, 2), :, later], osnd.at[2])
        drain(G.at[:, 0, 0, :, later], osnd.at[3])

    def left():
        drain(R, osnd.at[4])
        drain(B, osnd.at[5])
        drain(R, osnd.at[6])
        for at, ref in enumerate((RK, SY, RQ, ZK, SZ, ZQ)):
            drain(ref, osnd.at[7 + at])
        drain(KV.at[:, 0, pl.ds(0, NZ - 1)], osnd.at[13])

    steps = dict(
        gz=gather_z, gy=gather_y, ge=gather_end, ry=rest_y, rf=rest_far, rz=rest_z, dp=down_project, bd=boundary,
        sp=spread, pp=project_pairs, pq=project_queries, ky=sum_pairs_y, qy=sum_queries_y, kz=sum_pairs_z,
        qz=sum_queries_z, py=pairs_y, pe=pairs_end, at=attend,
    )
    for at, (name, *which) in enumerate(ORDER):
        if at == LOADED:
            for copy in local[1:]:
                copy.wait()
        if at == GATHERED:
            gathered()
        if at == LEFT:
            left()
        steps[name](*which)
    drain(KV.at[:, pl.ds(0, NY - 1)], osnd.at[14])


def per_device(hidden, down_weight, residual, norm_gain, query_weight, key_value_weight):
    own_rows, ff = hidden.shape[1:]
    feats = down_weight.shape[2]
    positions = (lax.axis_index("tensor") * own_rows + jnp.arange(own_rows, dtype=jnp.int32)).astype(F32)
    frequency = ROPE_BASE ** (-jnp.arange(HD // 2, dtype=F32) * 2.0 / HD)
    angles = positions[:, None] * frequency[None, :]
    cosine, sine = jnp.cos(angles), jnp.sin(angles)
    ctab = jnp.concatenate([cosine, cosine], axis=1)
    stab = jnp.concatenate([-sine, sine], axis=1)
    chunk = NY * NZ * ROWS
    dma = pltpu.SemaphoreType.DMA
    vmem = pl.BlockSpec(memory_space=pltpu.VMEM)
    hbm = pl.BlockSpec(memory_space=pltpu.HBM)
    attended = pl.pallas_call(
        kernel,
        out_shape=jax.ShapeDtypeStruct((own_rows, 512), BF),
        in_specs=[hbm] * 8,
        out_specs=vmem,
        scratch_shapes=[
            pltpu.VMEM((2, NK, ROWS, feats), BF),
            pltpu.VMEM((1, feats), F32),
            pltpu.VMEM((own_rows, HD), F32),
            pltpu.VMEM((own_rows, HD), F32),
            pltpu.VMEM((4 * own_rows, 1), F32),
            pltpu.VMEM((4 * own_rows, 1), F32),
            pltpu.VMEM((4 * own_rows, HD), F32),
            pltpu.VMEM((NK, NY, NZ, ROWS, ff), BF),
            pltpu.VMEM((ff, feats), BF),
            pltpu.VMEM((feats, 768), BF),
            pltpu.VMEM((chunk, feats), F32),
            pltpu.VMEM((NK, NY, NZ, ROWS, feats), BF),
            pltpu.VMEM((NK, ND - 1, 2, ROWS, feats), BF),
            pltpu.VMEM((NK, 2, ROWS, feats), BF),
            pltpu.VMEM((NK, NZ, 2, 2, ROWS, feats), BF),
            pltpu.VMEM((NK, chunk, feats), BF),
            pltpu.VMEM((NK, NZ, 2, 2, ROWS, 256), BF),
            pltpu.VMEM((NK, NZ, 2, 2, ROWS, 512), BF),
            pltpu.VMEM((NK, NY - 1, NZ, ROWS, 256), BF),
            pltpu.VMEM((NK, NY - 1, NZ, ROWS, 512), BF),
            pltpu.VMEM((NK, NZ, ROWS, 256), BF),
            pltpu.VMEM((NK, NZ, ROWS, 512), BF),
            pltpu.VMEM((NK, NZ - 1, ROWS, 256), BF),
            pltpu.VMEM((NK, NZ - 1, ROWS, 512), BF),
            pltpu.VMEM((NK, 8, chunk), F32),
            pltpu.VMEM((NK, NY - 1, 8, chunk), F32),
            pltpu.VMEM((NK, 8, chunk), F32),
            pltpu.VMEM((NK, NZ - 1, 8, chunk), F32),
            pltpu.VMEM((NK, ROWS, HD), F32),
            pltpu.VMEM((4, own_rows, HD), BF),
            pltpu.VMEM((NK, NY, NZ, ROWS, 2 * HD), BF),
            dma((8,)),
            dma((4,)),
            dma((15,)),
            dma((NK, NZ)), dma((NK, NZ, 2)), dma((NK,)), dma((NK, 2)), dma((NK,)), dma((NK, NZ)),
            dma((NK,)), dma((NK,)), dma((NK,)), dma((NK,)), dma((NK,)), dma((NK,)),
            dma((NK,)), dma((NK,)), dma((NK,)), dma((NK,)), dma((NK,)),
        ],
        compiler_params=pltpu.CompilerParams(collective_id=0, has_side_effects=True, vmem_limit_bytes=62 << 20),
    )(
        hidden.reshape(NK, ROWS, ff),
        down_weight[0],
        query_weight[0],
        key_value_weight[0],
        residual.reshape(2, NK, ROWS, feats),
        norm_gain,
        ctab,
        stab,
    )
    return attended[None]


def solution(mesh):
    placed = (
        P("section", "tensor", "dp"),
        P("section", "dp", "tensor"),
        P("section", "dp", "tensor"),
        P("section", "tensor"),
        P("section", "tensor", "dp"),
        P("section", "tensor", "dp"),
    )
    return jax.shard_map(
        per_device,
        mesh=mesh,
        in_specs=placed,
        out_specs=P("section", "tensor", "dp"),
        check_vma=False,
    )
```

```python
import jax
import jax.numpy as jnp
from jax import lax
from jax.experimental import pallas as pl
from jax.experimental.pallas import tpu as pltpu
from jax.sharding import PartitionSpec as P

D = 8192
HD = 128
ROPE_BASE = 500000.0
EPSILON = 1e-05

MESH = pl.DeviceIdType.MESH
NZ, NY, ND, NS = 4, 4, 8, 4
NK = 4
ROWS = 16
BF = jnp.bfloat16
F32 = jnp.float32


COLS = 24
ORDER = [
    ("ry", 3), ("ry", 0), ("ry", 1), ("ry", 2), ("gz", 0, 0), ("rf", 1), ("rf", 3), ("gz", 1, 0),
    ("gz", 0, 1), ("rf", 0), ("gz", 2, 0), ("gz", 2, 1), ("rz", 0, 0), ("gz", 1, 1), ("gz", 0, 2), ("gz", 0, 3),
    ("rz", 0, 1), ("rf", 2), ("gz", 2, 2), ("gy", 0, 0), ("gy", 0, 1), ("rz", 1, 0), ("rz", 0, 2), ("gz", 2, 3),
    ("rz", 2, 0), ("rz", 1, 1), ("rz", 0, 3), ("gy", 2, 0), ("gy", 2, 1), ("gy", 0, 2), ("gy", 0, 3), ("rz", 1, 2),
    ("gz", 1, 2), ("rz", 3, 0), ("rz", 2, 1), ("gz", 3, 0), ("gy", 2, 2), ("ge", 0), ("gy", 2, 3), ("dp", 0),
    ("gz", 1, 3), ("rz", 3, 1), ("gy", 1, 0), ("gy", 1, 1), ("rz", 1, 3), ("gy", 1, 2), ("gz", 3, 1), ("rz", 2, 2),
    ("rz", 2, 3), ("ge", 2), ("bd", 0), ("dp", 2), ("gy", 1, 3), ("gz", 3, 2), ("gz", 3, 3), ("sp", 0),
    ("gy", 3, 0), ("bd", 2), ("gy", 3, 1), ("ge", 1), ("dp", 1), ("rz", 3, 2), ("rz", 3, 3), ("gy", 3, 2),
    ("gy", 3, 3), ("pp", 0), ("sp", 2), ("bd", 1), ("ge", 3), ("dp", 3), ("pq", 0), ("sp", 1),
    ("pp", 2), ("bd", 3), ("pq", 2), ("pp", 1), ("ky", 0), ("ky", 2), ("pq", 1), ("sp", 3),
    ("qy", 2), ("qy", 0), ("ky", 1), ("kz", 0), ("qy", 1), ("kz", 2), ("pp", 3), ("pq", 3),
    ("py", 0), ("kz", 1), ("ky", 3), ("py", 2), ("pe", 0), ("qy", 3), ("py", 1), ("kz", 3),
    ("py", 3), ("qz", 1), ("pe", 1), ("qz", 0), ("qz", 2), ("qz", 3), ("at", 0, 2), ("pe", 2),
    ("at", 2, 3), ("pe", 3), ("at", 3, 4),
]
LOADED = min(ORDER.index(("dp", k)) for k in range(NK))
GATHERED = ORDER.index(("sp", 3))
LEFT = ORDER.index(("at", 3, 4)) - 1


def kernel(
    hid, w_hbm, wq_hbm, wkv_hbm, res_hbm, gain_hbm, ctab_hbm, stab_hbm, out,
    res, gain, ctab, stab, peak, mass, mixed,
    G, W, WP, acc, Pb, R, B, E, XS, UK, UQ, RK, RQ, VK, VQ, ZK, ZQ, SQ, SY, SV, SZ, inv, Qb, KV,
    lsem, zsnd, osnd,
    zrcv, yrcv, frcv, byrcv, bfrcv, bzrcv,
    drcv, srcv, grcv, ukrcv, uqrcv, vkrcv,
    vqrcv, qyrcv, qzrcv, kzrcv, kyrcv,
):
    s = lax.axis_index("section")
    d = lax.axis_index("dp")
    t = lax.axis_index("tensor")
    z, y = t // NY, t % NY
    ff, feats = W.shape
    first_cols = ff * COLS // 28
    half = first_cols // 2
    rest = ff - first_cols
    near, later = pl.ds(0, first_cols), pl.ds(first_cols, rest)
    inner = jnp.logical_and(z > 0, z < NZ - 1)

    def at_z(zz):
        return (s, d, zz * NY + y)

    def at_y(yy):
        return (s, d, z * NY + yy)

    def at_d(dd):
        return (s, dd, t)

    def piece(i):
        return (z, z + 1 - 2 * (z % 2), 2 - z // 2, 3 - 3 * (z // 2))[i]

    def remote(src, dst, snd, rcv, where):
        return pltpu.make_async_remote_copy(
            src_ref=src, dst_ref=dst, send_sem=snd, recv_sem=rcv, device_id=where, device_id_type=MESH
        )

    def send(copy, cond=None):
        if cond is None:
            copy.start()
        else:
            pl.when(cond)(copy.start)

    def drain(ref, sem):
        pltpu.make_async_copy(ref, ref, sem).wait()

    local = [
        pltpu.make_async_copy(hid, G.at[:, y, z], lsem.at[0]),
        pltpu.make_async_copy(w_hbm, W, lsem.at[1]),
        pltpu.make_async_copy(wq_hbm, WP.at[:, pl.ds(0, 512)], lsem.at[2]),
        pltpu.make_async_copy(wkv_hbm, WP.at[:, pl.ds(512, 256)], lsem.at[3]),
        pltpu.make_async_copy(res_hbm, res, lsem.at[4]),
        pltpu.make_async_copy(gain_hbm, gain, lsem.at[5]),
        pltpu.make_async_copy(ctab_hbm, ctab, lsem.at[6]),
        pltpu.make_async_copy(stab_hbm, stab, lsem.at[7]),
    ]
    for copy in local:
        copy.start()

    barrier = pltpu.get_barrier_semaphore()
    peers = [at_y((y + j) % NY) for j in range(1, NY)]
    peers += [at_z((z + j) % NZ) for j in range(1, NZ)]
    peers += [at_d((d + j) % ND) for j in range(1, ND)]
    peers += [((s + 1) % NS, d, t), ((s + NS - 1) % NS, d, t)]
    for peer in peers:
        pl.semaphore_signal(barrier, inc=1, device_id=peer, device_id_type=MESH)
    pl.semaphore_wait(barrier, len(peers))
    local[0].wait()

    up, down = (y + 1) % NY, (y + NY - 1) % NY

    def gather_z(k, i):
        zp = piece(i)
        own = G.at[k, y, zp, :, near]
        if i == 0:
            send(remote(own, own, zsnd.at[0], zrcv.at[k, zp], at_z(jnp.minimum(z + 1, NZ - 1))), z < NZ - 1)
            send(remote(own, own, zsnd.at[0], zrcv.at[k, zp], at_z(jnp.maximum(z - 1, 0))), z > 0)
        else:
            target = 3 - z if i == 1 else 3 * (z // 2)
            relay = remote(own, own, zsnd.at[1], zrcv.at[k, zp], at_z(target))
            relay.wait_recv()
            send(relay, inner)
        send(remote(own, own, osnd.at[0], yrcv.at[k, i, 0], at_y(up)))
        send(remote(own, own, osnd.at[0], yrcv.at[k, i, 1], at_y(down)))

    def gather_y(k, i):
        zp = piece(i)
        for way, source, target, first in ((0, down, up, 0), (1, up, down, half)):
            whole = G.at[k, source, zp, :, near]
            drain(whole, yrcv.at[k, i, way])
            part = G.at[k, source, zp, :, pl.ds(first, half)]
            send(remote(part, part, osnd.at[1], frcv.at[k], at_y(target)))

    def gather_end(k):
        drain(G.at[k, (y + 2) % NY, :, :, near], frcv.at[k])

    def rest_y(k):
        own = G.at[k, y, z, :, later]
        send(remote(own, own, osnd.at[2], byrcv.at[k, 0], at_y(up)))
        send(remote(own, own, osnd.at[2], byrcv.at[k, 1], at_y(down)))

    def rest_far(k):
        for way, source, target, first in ((0, down, up, 0), (1, up, down, rest // 2)):
            whole = G.at[k, source, z, :, later]
            drain(whole, byrcv.at[k, way])
            part = G.at[k, source, z, :, pl.ds(first_cols + first, rest // 2)]
            send(remote(part, part, osnd.at[3], bfrcv.at[k], at_y(target)))

    def rest_z(k, i):
        zp = piece(i)
        own = G.at[k, :, zp, :, later]
        if i == 0:
            drain(G.at[k, (y + 2) % NY, z, :, later], bfrcv.at[k])
            send(remote(own, own, zsnd.at[2], bzrcv.at[k, zp], at_z(jnp.minimum(z + 1, NZ - 1))), z < NZ - 1)
            send(remote(own, own, zsnd.at[2], bzrcv.at[k, zp], at_z(jnp.maximum(z - 1, 0))), z > 0)
        else:
            target = 3 - z if i == 1 else 3 * (z // 2)
            relay = remote(own, own, zsnd.at[3], bzrcv.at[k, zp], at_z(target))
            relay.wait_recv()
            send(relay, inner)

    def down_project(k):
        depth = ff // 4
        for n in range(4):
            g = G[k, :, :, :, n * depth:(n + 1) * depth].reshape(NY * NZ * ROWS, depth)
            part = jnp.dot(g, W[n * depth:(n + 1) * depth, :], preferred_element_type=F32)
            if n == 0:
                acc[...] = part
            elif n < 3:
                acc[...] += part
            else:
                Pb[k] = (acc[...] + part).astype(BF).reshape(NY, NZ, ROWS, feats)
        for j in range(1, ND):
            dd = (d + j) % ND
            send(remote(Pb.at[k, pl.ds(2 * (dd % 2), 2), dd // 2], R.at[k, j - 1], osnd.at[4], drcv.at[k], at_d(dd)))

    def boundary(k):
        total = res[:, k].astype(F32) + Pb[k, pl.ds(2 * (d % 2), 2), d // 2].astype(F32)
        drain(R.at[k], drcv.at[k])
        for j in range(ND - 1):
            total = total + R[k, j].astype(F32)
        B[k] = total.astype(BF)
        send(remote(B.at[k], E.at[k, d // 2, d % 2], osnd.at[5], srcv.at[k], ((s + 1) % NS, d, t)))

    def spread(k):
        own = E.at[k, d // 2, d % 2]
        drain(own, srcv.at[k])
        for j in range(1, ND):
            send(remote(own, own, osnd.at[6], grcv.at[k], at_d((d + j) % ND)))

    def project_pairs(k):
        drain(R.at[k], grcv.at[k])
        x = E[k].reshape(NY * NZ * ROWS, feats).astype(F32)
        scaled = (x * gain[...]).astype(BF)
        XS[k] = scaled
        UK[k] = jnp.dot(scaled, WP[:, 512:768], preferred_element_type=F32).astype(BF).reshape(NZ, 2, 2, ROWS, 256)
        squares = lax.dot_general(
            jnp.ones((8, feats), BF), (x * x).astype(BF), (((1,), (1,)), ((), ())), preferred_element_type=F32
        )
        lower = lax.broadcasted_iota(jnp.int32, (8, HD), 0) == 0
        SQ[k] = jnp.where(lower, squares[:, 0:HD], squares[:, HD:2 * HD])
        for j in range(1, NY):
            yy = (y + j) % NY
            send(remote(UK.at[k, :, yy // 2, yy % 2], RK.at[k, j - 1], osnd.at[7], ukrcv.at[k], at_y(yy)))
            send(remote(SQ.at[k], SY.at[k, j - 1], osnd.at[8], qyrcv.at[k], at_y(yy)))

    def project_queries(k):
        UQ[k] = jnp.dot(XS[k], WP[:, 0:512], preferred_element_type=F32).astype(BF).reshape(NZ, 2, 2, ROWS, 512)
        for j in range(1, NY):
            yy = (y + j) % NY
            send(remote(UQ.at[k, :, yy // 2, yy % 2], RQ.at[k, j - 1], osnd.at[9], uqrcv.at[k], at_y(yy)))

    def sum_pairs_y(k):
        drain(RK.at[k], ukrcv.at[k])
        drain(SY.at[k], qyrcv.at[k])
        total = UK[k, :, y // 2, y % 2].astype(F32)
        squares = SQ[k]
        for j in range(1, NY):
            total = total + RK[k, j - 1].astype(F32)
            squares = squares + SY[k, j - 1]
        VK[k] = total.astype(BF)
        SV[k] = squares
        for j in range(1, NZ):
            zz = (z + j) % NZ
            send(remote(VK.at[k, zz], ZK.at[k, j - 1], osnd.at[10], vkrcv.at[k], at_z(zz)))
            send(remote(SV.at[k], SZ.at[k, j - 1], osnd.at[11], qzrcv.at[k], at_z(zz)))

    def sum_queries_y(k):
        drain(RQ.at[k], uqrcv.at[k])
        total = UQ[k, :, y // 2, y % 2].astype(F32)
        for j in range(1, NY):
            total = total + RQ[k, j - 1].astype(F32)
        VQ[k] = total.astype(BF)
        for j in range(1, NZ):
            zz = (z + j) % NZ
            send(remote(VQ.at[k, zz], ZQ.at[k, j - 1], osnd.at[12], vqrcv.at[k], at_z(zz)))

    def rotate(u, k):
        rows = pl.ds(k * ROWS, ROWS)
        return (u * ctab[rows, :] + pltpu.roll(u, HD // 2, 1) * stab[rows, :]).astype(BF)

    def sum_pairs_z(k):
        drain(ZK.at[k], vkrcv.at[k])
        drain(SZ.at[k], qzrcv.at[k])
        total = VK[k, z].astype(F32)
        squares = SV[k]
        for j in range(1, NZ):
            total = total + ZK[k, j - 1].astype(F32)
            squares = squares + SZ[k, j - 1]
        tokens = NY * NZ * ROWS
        lane = lax.broadcasted_iota(jnp.int32, (ROWS, tokens), 1)
        row = lax.broadcasted_iota(jnp.int32, (ROWS, tokens), 0)
        row_squares = jnp.concatenate(
            [jnp.broadcast_to(squares[0:1, :], (ROWS, HD)), jnp.broadcast_to(squares[1:2, :], (ROWS, HD))], axis=1
        )
        own_squares = jnp.sum(jnp.where(lane == row + t * ROWS, row_squares, 0.0), axis=1, keepdims=True)
        inverse = lax.rsqrt(own_squares / D + EPSILON)
        inv[k] = jnp.broadcast_to(inverse, (ROWS, HD))
        KV[k, y, z, :, 0:HD] = rotate(total[:, 0:HD] * inverse, k)
        KV[k, y, z, :, HD:2 * HD] = (total[:, HD:2 * HD] * inverse).astype(BF)
        own = KV.at[k, y, z]
        for j in range(1, NY):
            send(remote(own, own, osnd.at[13], kyrcv.at[k], at_y((y + j) % NY)))

    def sum_queries_z(k):
        drain(ZQ.at[k], vqrcv.at[k])
        total = VQ[k, z].astype(F32)
        for j in range(1, NZ):
            total = total + ZQ[k, j - 1].astype(F32)
        for h in range(4):
            Qb[h, k * ROWS:(k + 1) * ROWS, :] = rotate(total[:, h * HD:(h + 1) * HD] * inv[k], k)

    def pairs_z(k):
        drain(KV.at[k, pl.ds(0, NY - 1), z], kyrcv.at[k])
        own = KV.at[k, :, z]
        for j in range(1, NZ):
            send(remote(own, own, osnd.at[14], kzrcv.at[k], at_z((z + j) % NZ)))

    def pairs_end(k):
        drain(KV.at[k, :, pl.ds(0, NZ - 1)], kzrcv.at[k])

    def attend(first, last):
        tokens = (last - first) * NY * NZ * ROWS
        queries = Qb[...].reshape(4 * 64, HD)
        keys = KV[first:last, :, :, :, 0:HD].reshape(tokens, HD)
        values = KV[first:last, :, :, :, HD:2 * HD].reshape(tokens, HD)
        scores = lax.dot_general(queries, keys, (((1,), (1,)), ((), ())), preferred_element_type=F32) * HD ** (-0.5)
        lane = lax.broadcasted_iota(jnp.int32, (1, tokens), 1) + first * NY * NZ * ROWS
        key_at = ((lane >> 4) & 3) * 256 + ((lane >> 6) & 3) * 64 + (lane >> 8) * 16 + (lane & 15)
        row = lax.broadcasted_iota(jnp.int32, (256, 1), 0)
        query_at = (row & 63) + t * 64
        scores = jnp.where(key_at <= query_at, scores, -1e30)
        top = jnp.max(scores, axis=1, keepdims=True)
        if first > 0:
            top = jnp.maximum(top, peak[...])
        weights = jnp.exp(scores - top)
        total = jnp.sum(weights, axis=1, keepdims=True)
        result = jnp.dot(weights.astype(BF), values, preferred_element_type=F32)
        if first > 0:
            fade = jnp.exp(peak[...] - top)
            total = total + mass[...] * fade
            result = result + mixed[...] * fade
        if last < NK:
            peak[...] = top
            mass[...] = total
            mixed[...] = result
        else:
            result = (result / total).astype(BF)
            for h in range(4):
                out[:, h * HD:(h + 1) * HD] = result[h * 64:(h + 1) * 64, :]

    def gathered():
        @pl.when(inner)
        def _():
            drain(G.at[:, 0, pl.ds(0, 2), :, near], zsnd.at[0])
            drain(G.at[:, 0, pl.ds(0, 3), :, near], zsnd.at[1])
            drain(G.at[:, pl.ds(0, 2), :, :, later], zsnd.at[2])
            drain(G.at[:, pl.ds(0, 3), :, :, later], zsnd.at[3])

        @pl.when(jnp.logical_not(inner))
        def _():
            drain(G.at[:, 0, 0, :, near], zsnd.at[0])
            drain(G.at[:, 0, :, :, later], zsnd.at[2])

        drain(G.at[:, pl.ds(0, 2), :, :, near], osnd.at[0])
        drain(G.at[:, 0, :, :, near], osnd.at[1])
        drain(G.at[:, 0, pl.ds(0, 2), :, later], osnd.at[2])
        drain(G.at[:, 0, 0, :, later], osnd.at[3])

    def left():
        drain(R, osnd.at[4])
        drain(B, osnd.at[5])
        drain(R, osnd.at[6])
        for at, ref in enumerate((RK, SY, RQ, ZK, SZ, ZQ)):
            drain(ref, osnd.at[7 + at])
        drain(KV.at[:, pl.ds(0, NY - 1), 0], osnd.at[13])

    steps = dict(
        gz=gather_z, gy=gather_y, ge=gather_end, ry=rest_y, rf=rest_far, rz=rest_z, dp=down_project, bd=boundary,
        sp=spread, pp=project_pairs, pq=project_queries, ky=sum_pairs_y, qy=sum_queries_y, kz=sum_pairs_z,
        qz=sum_queries_z, py=pairs_z, pe=pairs_end, at=attend,
    )
    for at, (name, *which) in enumerate(ORDER):
        if at == LOADED:
            for copy in local[1:]:
                copy.wait()
        if at == GATHERED:
            gathered()
        if at == LEFT:
            left()
        steps[name](*which)
    drain(KV.at[:, :, pl.ds(0, NZ - 1)], osnd.at[14])


def per_device(hidden, down_weight, residual, norm_gain, query_weight, key_value_weight):
    own_rows, ff = hidden.shape[1:]
    feats = down_weight.shape[2]
    positions = (lax.axis_index("tensor") * own_rows + jnp.arange(own_rows, dtype=jnp.int32)).astype(F32)
    frequency = ROPE_BASE ** (-jnp.arange(HD // 2, dtype=F32) * 2.0 / HD)
    angles = positions[:, None] * frequency[None, :]
    cosine, sine = jnp.cos(angles), jnp.sin(angles)
    ctab = jnp.concatenate([cosine, cosine], axis=1)
    stab = jnp.concatenate([-sine, sine], axis=1)
    chunk = NY * NZ * ROWS
    dma = pltpu.SemaphoreType.DMA
    vmem = pl.BlockSpec(memory_space=pltpu.VMEM)
    hbm = pl.BlockSpec(memory_space=pltpu.HBM)
    attended = pl.pallas_call(
        kernel,
        out_shape=jax.ShapeDtypeStruct((own_rows, 512), BF),
        in_specs=[hbm] * 8,
        out_specs=vmem,
        scratch_shapes=[
            pltpu.VMEM((2, NK, ROWS, feats), BF),
            pltpu.VMEM((1, feats), F32),
            pltpu.VMEM((own_rows, HD), F32),
            pltpu.VMEM((own_rows, HD), F32),
            pltpu.VMEM((4 * own_rows, 1), F32),
            pltpu.VMEM((4 * own_rows, 1), F32),
            pltpu.VMEM((4 * own_rows, HD), F32),
            pltpu.VMEM((NK, NY, NZ, ROWS, ff), BF),
            pltpu.VMEM((ff, feats), BF),
            pltpu.VMEM((feats, 768), BF),
            pltpu.VMEM((chunk, feats), F32),
            pltpu.VMEM((NK, NY, NZ, ROWS, feats), BF),
            pltpu.VMEM((NK, ND - 1, 2, ROWS, feats), BF),
            pltpu.VMEM((NK, 2, ROWS, feats), BF),
            pltpu.VMEM((NK, NZ, 2, 2, ROWS, feats), BF),
            pltpu.VMEM((NK, chunk, feats), BF),
            pltpu.VMEM((NK, NZ, 2, 2, ROWS, 256), BF),
            pltpu.VMEM((NK, NZ, 2, 2, ROWS, 512), BF),
            pltpu.VMEM((NK, NY - 1, NZ, ROWS, 256), BF),
            pltpu.VMEM((NK, NY - 1, NZ, ROWS, 512), BF),
            pltpu.VMEM((NK, NZ, ROWS, 256), BF),
            pltpu.VMEM((NK, NZ, ROWS, 512), BF),
            pltpu.VMEM((NK, NZ - 1, ROWS, 256), BF),
            pltpu.VMEM((NK, NZ - 1, ROWS, 512), BF),
            pltpu.VMEM((NK, 8, chunk // 2), F32),
            pltpu.VMEM((NK, NY - 1, 8, chunk // 2), F32),
            pltpu.VMEM((NK, 8, chunk // 2), F32),
            pltpu.VMEM((NK, NZ - 1, 8, chunk // 2), F32),
            pltpu.VMEM((NK, ROWS, HD), F32),
            pltpu.VMEM((4, own_rows, HD), BF),
            pltpu.VMEM((NK, NY, NZ, ROWS, 2 * HD), BF),
            dma((8,)),
            dma((4,)),
            dma((15,)),
            dma((NK, NZ)), dma((NK, NZ, 2)), dma((NK,)), dma((NK, 2)), dma((NK,)), dma((NK, NZ)),
            dma((NK,)), dma((NK,)), dma((NK,)), dma((NK,)), dma((NK,)), dma((NK,)),
            dma((NK,)), dma((NK,)), dma((NK,)), dma((NK,)), dma((NK,)),
        ],
        compiler_params=pltpu.CompilerParams(collective_id=0, has_side_effects=True, vmem_limit_bytes=62 << 20),
    )(
        hidden.reshape(NK, ROWS, ff),
        down_weight[0],
        query_weight[0],
        key_value_weight[0],
        residual.reshape(2, NK, ROWS, feats),
        norm_gain,
        ctab,
        stab,
    )
    return attended[None]


def solution(mesh):
    placed = (
        P("section", "tensor", "dp"),
        P("section", "dp", "tensor"),
        P("section", "dp", "tensor"),
        P("section", "tensor"),
        P("section", "tensor", "dp"),
        P("section", "tensor", "dp"),
    )
    return jax.shard_map(
        per_device,
        mesh=mesh,
        in_specs=placed,
        out_specs=P("section", "tensor", "dp"),
        check_vma=False,
    )
```
